256 devices in a mesh: wide: 32 (over y, x, core), narrow: 8 (over z).
Axes of the slice: x: 4, y: 4, z: 8, core: 2. Of those that a mesh axis runs over, the one named last changes fastest.
Arguments:
- three_centre: bfloat16 [32, 1024, 4096], P('narrow', 'wide'), may hold values from -6 to 6
- go_blocks: bfloat16 [64, 64, 64], replicated, may hold values from -0.75 to 0.75
- gv_blocks: bfloat16 [64, 64, 64], replicated, may hold values from -0.125 to 0.125
- go_index: int32 [32, 32], P('narrow'), may hold values from 0 to 63
- gv_index: int32 [32, 32], P('narrow'), may hold values from 0 to 63
- source_mask: int32 [32, 32], P('narrow'), may hold values 0 or 1
Outputs:
- chi: float32 [1024, 1024], P('wide', 'narrow')
The draws below stay inside these ranges and needn't reach their ends.
All inputs are finite; a program needn't handle non-finite values. No bound on the sum of `source_mask` on one device may be relied on, other than what follows from the above.
Results may differ from the reference program's by a relative error of at most 0.004.
Values may be sent and summed in bfloat16 or wider, within the bound.
No kernel may reach another device: no remote copies, remote signals or barrier semaphores. Data moves between devices by JAX's collectives and lax.ppermute only.
A program may use at most 192 MiB of HBM per device.

```python
import jax
import jax.numpy as jnp
from jax import lax

BLK = 64
PAIRS = 4096
AUX = 1024
NPAIR = 32
NGB = 64


def touch_ends(array, stream_key, low, high):
    place = [jax.random.randint(jax.random.fold_in(stream_key, axis), (), 0, length) for axis, length in enumerate(array.shape)]
    main_axis = array.shape.index(max(array.shape))
    next_to = place[:main_axis] + [(place[main_axis] + 1) % array.shape[main_axis]] + place[main_axis + 1:]
    return array.at[tuple(place)].set(low).at[tuple(next_to)].set(high)


def levels(own_key, extent, cuts, low, largest):
    level, own = 1.0, jax.random.fold_in(own_key, 6)
    for axis_at, parts in cuts:
        heights = jnp.exp(jax.random.uniform(jax.random.fold_in(own, axis_at), (parts,), jnp.float32, low / len(cuts), largest / len(cuts)))
        level = level * jnp.repeat(heights, extent[axis_at] // parts).reshape([-1 if axis == axis_at else 1 for axis in range(len(extent))])
    return level


def noise(own_key, extent, scale, most, split=(), kind=jnp.bfloat16):
    result = jax.random.normal(own_key, extent, jnp.float32) * scale
    if len(split) > 0:
        result = levels(own_key, extent, split, -0.22, 0.18) * result
    return jnp.clip(result, min=-most, max=most).astype(kind)


def setup_inputs(seed: int = 0) -> dict:
    streams_of = jax.random.split(jax.random.key(seed), 7)
    return {
        "three_centre": noise(streams_of[0], (NPAIR, AUX, PAIRS), 1.0, 6.0, ((0, 8), (1, 32))),
        "go_blocks": noise(streams_of[1], (NGB, BLK, BLK), BLK ** -0.5, 0.75),
        "gv_blocks": noise(streams_of[2], (NGB, BLK, BLK), (BLK * NPAIR) ** -0.5, 0.125),
        "go_index": touch_ends(jax.random.randint(streams_of[3], (NPAIR, NPAIR), 0, NGB), jax.random.fold_in(streams_of[3], 1), 0, NGB - 1).astype(jnp.int32),
        "gv_index": touch_ends(jax.random.randint(streams_of[4], (NPAIR, NPAIR), 0, NGB), jax.random.fold_in(streams_of[4], 1), 0, NGB - 1).astype(jnp.int32),
        "source_mask": touch_ends((jax.random.randint(streams_of[5], (NPAIR, NPAIR), 0, 3) < 2).astype(jnp.int32), jax.random.fold_in(streams_of[5], 1), 0, 1),
    }


def reference(three_centre, go_blocks, gv_blocks, go_index, gv_index, source_mask):
    npair = three_centre.shape[0]
    blocks = three_centre.reshape(npair, AUX, BLK, BLK)

    def one_target(inputs):
        go_row, gv_row, mask_row = inputs

        def one_source(total, index):
            go_block = go_blocks[go_row[index]].astype(jnp.float32)
            gv_block = (gv_blocks[gv_row[index]] * mask_row[index].astype(jnp.bfloat16)).astype(jnp.float32)
            first = jnp.einsum('ma,pmn->pan', go_block, blocks[index].astype(jnp.float32)).astype(jnp.bfloat16)
            return (total + jnp.einsum('pan,nd->pad', first.astype(jnp.float32), gv_block), None)
        total, unused = lax.scan(one_source, jnp.zeros((AUX, BLK, BLK), jnp.float32), jnp.arange(npair, dtype=jnp.int32))
        return total.astype(jnp.bfloat16)
    image = lax.map(one_target, (go_index, gv_index, source_mask)).reshape(npair, AUX, PAIRS)
    partial_chi = jnp.einsum('kpe,kqe->pq', image.astype(jnp.float32), three_centre.astype(jnp.float32))
    return partial_chi / jnp.sqrt(jnp.float32(NPAIR * PAIRS))
```

```python
import functools

import jax
import jax.numpy as jnp
from jax import lax
from jax.experimental import pallas as pl
from jax.experimental.pallas import tpu as pltpu
from jax.sharding import Mesh, PartitionSpec as P

WIDE = ("y", "x", "core")
LANES = 128
BLK = 64
VMEM = pltpu.VMEM
SMEM = pltpu.SMEM


def vmem(n):
    return [pl.BlockSpec(memory_space=VMEM)] * n


def pair_halves(first, second):
    left = lax.broadcasted_iota(jnp.int32, first.shape, 1) < BLK
    low = jnp.where(left, first, pltpu.roll(second, BLK, 1))
    high = jnp.where(left, pltpu.roll(first, BLK, 1), second)
    return low, high


def spread_kernel(c_ref, code_ref, out_ref):
    pairs, aux, width = c_ref.shape
    half = width // LANES
    for j in range(pairs):
        for g in range(aux // 16):
            x = c_ref[j, 16 * g : 16 * g + 16, :].astype(jnp.float32)
            x = pltpu.einshape("p(tl)->ptl", x, l=LANES)
            for i in range(4):
                low01, high01 = pair_halves(x[4 * i], x[4 * i + 1])
                low23, high23 = pair_halves(x[4 * i + 2], x[4 * i + 3])
                d = 4 * g + i
                r = 2 * half * j
                out_ref[d, r : r + half, :LANES] = low01.astype(jnp.bfloat16)
                out_ref[d, r : r + half, LANES:] = low23.astype(jnp.bfloat16)
                out_ref[d, r + half : r + 2 * half, :LANES] = high01.astype(jnp.bfloat16)
                out_ref[d, r + half : r + 2 * half, LANES:] = high23.astype(jnp.bfloat16)
    rows = pairs * 2 * half
    for d in range(aux // 4):
        out_ref[d, rows : rows + 16, :] = code_ref[...]


def image_kernel(go_code, gv_code, w_ref, gt_ref, vb_ref, out_ref, stage):
    nsrc = w_ref.shape[0]
    pairs = 4
    number = nsrc * pairs
    step = 8

    @pl.loop(0, nsrc)
    def _(zd):
        for kk in range(pairs):
            k = zd * pairs + kk
            acc = None
            for jb in range(0, number, step):
                lefts, rights = [], []
                for j in range(jb, jb + step):
                    g = go_code[k, j]
                    v = gv_code[k, j]
                    r = BLK * (j % pairs)
                    first = jnp.dot(
                        gt_ref[g], w_ref[j // pairs, r : r + BLK, :], preferred_element_type=jnp.float32
                    ).astype(jnp.bfloat16)
                    lefts.append(jnp.concatenate([first[:, :LANES], first[:, LANES:]], axis=0))
                    rights.append(vb_ref[v])
                part = jnp.dot(
                    jnp.concatenate(lefts, axis=1),
                    jnp.concatenate(rights, axis=0),
                    preferred_element_type=jnp.float32,
                )
                acc = part if acc is None else acc + part
            for h in range(2):
                even, odd = acc[BLK * h : BLK * h + 32], acc[BLK * h + 32 : BLK * h + 64]
                p0, p1 = pair_halves(even, odd)
                stage[4 * kk + 2 * h] = p0
                stage[4 * kk + 2 * h + 1] = p1
        y = pltpu.einshape("ptl->p(tl)", stage[...]).astype(jnp.bfloat16)
        width = out_ref.shape[3]
        for xd in range(out_ref.shape[0]):
            out_ref[xd, zd] = y[:, width * xd : width * xd + width]


def chi_kernel(scale, ypos, im_ref, *refs):
    pieces, out_ref = refs[:-1], refs[-1]
    shifts = (0, 1, 3, 2)
    for s in range(4):
        own, other = pieces[2 * s], pieces[2 * s + 1]
        acc = None
        for k in range(4):
            rhs = jnp.concatenate(
                [ref[x, k] for x in range(4) for ref in (own, other)], axis=0
            )
            part = lax.dot_general(
                im_ref[k], rhs, (((1,), (1,)), ((), ())), preferred_element_type=jnp.float32
            )
            acc = part if acc is None else acc + part
        acc = (acc * scale).astype(jnp.bfloat16)
        y = lax.rem(ypos[0] + 4 - shifts[s], 4)
        for xd in range(4):
            for h in range(2):
                out_ref[xd, 2 * y + h] = acc[32 * xd : 32 * xd + 32, LANES * h : LANES * h + LANES]


def local(three_centre, go_blocks, gv_blocks, go_index, gv_index, source_mask):
    pairs, aux, width = three_centre.shape
    nz = lax.axis_size("z")
    nx = lax.axis_size("x")
    number = pairs * nz
    blocks = go_blocks.shape[0]
    scale = float((number * width) ** -0.5)

    codes = jnp.concatenate([go_index, jnp.where(source_mask != 0, gv_index, blocks)], axis=0)
    codes = jnp.broadcast_to(codes.astype(jnp.bfloat16).reshape(1, 2 * pairs * number), (16, 2 * pairs * number))
    rows = pairs * BLK
    spread = pl.pallas_call(
        spread_kernel,
        out_shape=jax.ShapeDtypeStruct((nz, rows + 16, 4 * BLK), jnp.bfloat16),
        in_specs=vmem(2),
        out_specs=vmem(1)[0],
        name="spread",
    )(three_centre, codes)
    w = lax.all_to_all(spread, "z", 0, 0, tiled=True)

    cx = three_centre.reshape(pairs, aux, nx, width // nx).transpose(2, 0, 1, 3)
    cx = lax.all_to_all(cx, "x", 0, 0, tiled=True)
    swap = [(0, 1), (1, 0)]
    pieces = []
    for s in (0, 1, 3, 2):
        own = cx if s == 0 else lax.ppermute(cx, "y", [(i, (i + s) % 4) for i in range(4)])
        pieces += [own, lax.ppermute(own, "core", swap)]

    gt = go_blocks.reshape(blocks, 32, 2, 32, 2).transpose(0, 4, 3, 2, 1).reshape(blocks, BLK, BLK)
    zero = jnp.zeros_like(gv_blocks)
    vb = jnp.concatenate(
        [jnp.concatenate([gv_blocks, zero], axis=2), jnp.concatenate([zero, gv_blocks], axis=2)], axis=1
    )
    vb = jnp.concatenate([vb, jnp.zeros((1, LANES, LANES), jnp.bfloat16)], axis=0)

    got = w[:, rows, :].astype(jnp.int32).reshape(nz, 2, pairs, number)
    go_code = got[:, 0].reshape(number, number)
    gv_code = got[:, 1].reshape(number, number)
    image = pl.pallas_call(
        image_kernel,
        out_shape=jax.ShapeDtypeStruct((nx, nz, 4 * pairs, width // nx), jnp.bfloat16),
        in_specs=[pl.BlockSpec(memory_space=SMEM)] * 2 + vmem(3),
        out_specs=vmem(1)[0],
        scratch_shapes=[VMEM((4 * pairs, width // LANES, LANES), jnp.float32)],
        name="image",
    )(go_code, gv_code, w, gt, vb)
    image = lax.all_to_all(image.reshape(nx * nz, 4 * pairs, width // nx), ("x", "z"), 0, 0, tiled=True)
    image = image.reshape(nx * nz, pairs, 4, width // nx).transpose(1, 0, 2, 3)
    image = image.reshape(pairs, nx * nz * 4, width // nx)

    part = pl.pallas_call(
        functools.partial(chi_kernel, scale),
        out_shape=jax.ShapeDtypeStruct((nx, nz, aux, 4 * aux), jnp.bfloat16),
        in_specs=[pl.BlockSpec(memory_space=SMEM)] + vmem(9),
        out_specs=vmem(1)[0],
        name="chi",
    )(lax.axis_index("y").reshape(1), image, *pieces)
    part = lax.all_to_all(part.reshape(nx * nz, aux, 4 * aux), ("x", "z"), 0, 0, tiled=True)
    chi = jnp.sum(part.astype(jnp.float32), axis=0).reshape(aux, 2, 2, aux)
    chi = jnp.where(lax.axis_index("core") == 0, chi, chi[:, :, ::-1])
    return chi.reshape(aux, 4 * aux)


def solution(mesh):
    grid = Mesh(mesh.devices.reshape(4, 4, 2, 8), WIDE + ("z",))
    rows = P("z", None)
    return jax.shard_map(
        local,
        mesh=grid,
        in_specs=(P("z", WIDE, None), P(), P(), rows, rows, rows),
        out_specs=P(WIDE, "z"),
        check_vma=False,
    )
```

```python
import functools

import jax
import jax.numpy as jnp
from jax import lax
from jax.experimental import pallas as pl
from jax.experimental.pallas import tpu as pltpu
from jax.sharding import Mesh, PartitionSpec as P

WIDE = ("y", "x", "core")
LANES = 128
BLK = 64
VMEM = pltpu.VMEM
SMEM = pltpu.SMEM
SHIFTS = (0, 1, 3, 2)


def vmem(n):
    return [pl.BlockSpec(memory_space=VMEM)] * n


def pair_halves(first, second):
    left = lax.broadcasted_iota(jnp.int32, first.shape, 1) < BLK
    low = jnp.where(left, first, pltpu.roll(second, BLK, 1))
    high = jnp.where(left, pltpu.roll(first, BLK, 1), second)
    return low, high


def spread_kernel(zero_code, c_hbm, go_hbm, gv_hbm, mask_hbm, out_ref, c_ref, ints, code, c_sem, int_sem):
    pairs, aux, width = c_ref.shape
    half = width // LANES
    loads = [pltpu.make_async_copy(c_hbm.at[j], c_ref.at[j], c_sem.at[j]) for j in range(pairs)]
    small = [pltpu.make_async_copy(ref, ints.at[i], int_sem.at[i]) for i, ref in enumerate((go_hbm, gv_hbm, mask_hbm))]
    for load in loads + small:
        load.start()
    for j in range(pairs):
        loads[j].wait()
        for g in range(aux // 16):
            x = c_ref[j, 16 * g : 16 * g + 16, :].astype(jnp.float32)
            x = pltpu.einshape("p(tl)->ptl", x, l=LANES)
            for i in range(4):
                d = 4 * g + i
                r = 2 * half * j
                for h in range(2):
                    one, two = x[4 * i + 2 * h], x[4 * i + 2 * h + 1]
                    low, high = pair_halves(one, two)
                    lanes = slice(LANES * h, LANES * h + LANES)
                    out_ref[d, r : r + half, lanes] = low.astype(jnp.bfloat16)
                    out_ref[d, r + half : r + 2 * half, lanes] = high.astype(jnp.bfloat16)
    rows = pairs * 2 * half
    number = ints.shape[2]
    for load in small:
        load.wait()
    code[...] = jnp.zeros_like(code)
    code[:pairs, :number] = ints[0].astype(jnp.float32)
    code[pairs : 2 * pairs, :number] = jnp.where(ints[2] != 0, ints[1], zero_code).astype(jnp.float32)
    for d in range(aux // 4):
        out_ref[d, rows : rows + 16, :] = code[...].astype(jnp.bfloat16)


def image_kernel(go_code, gv_code, w_ref, gt_ref, vb_ref, out_hbm, out_ref, sems):
    nsrc = w_ref.shape[0]
    pairs = out_ref.shape[1]
    number = nsrc * pairs
    step, batch = 4, 4

    @pl.loop(0, nsrc)
    def _(zd):
        for k0 in range(0, pairs, batch):
            ks = [zd * pairs + k0 + b for b in range(batch)]
            accs = [None] * batch
            for jb in range(0, number, step):
                lefts, rights = [[] for _ in ks], [[] for _ in ks]
                for j in range(jb, jb + step):
                    r = BLK * (j % pairs)
                    gt = [gt_ref[go_code[k, j]] for k in ks]
                    first = jnp.dot(
                        gt[0] if batch == 1 else jnp.concatenate(gt, axis=0),
                        w_ref[j // pairs, r : r + BLK, :],
                        preferred_element_type=jnp.float32,
                    ).astype(jnp.bfloat16)
                    for b, k in enumerate(ks):
                        own = first[BLK * b : BLK * b + BLK]
                        lefts[b].append(jnp.concatenate([own[:, :LANES], own[:, LANES:]], axis=0))
                        rights[b].append(vb_ref[gv_code[k, j]])
                for b in range(batch):
                    part = jnp.dot(
                        jnp.concatenate(lefts[b], axis=1),
                        jnp.concatenate(rights[b], axis=0),
                        preferred_element_type=jnp.float32,
                    )
                    accs[b] = part if accs[b] is None else accs[b] + part
            for b, acc in enumerate(accs):
                tiles = []
                for h in range(2):
                    tiles += pair_halves(acc[BLK * h : BLK * h + 32], acc[BLK * h + 32 : BLK * h + 64])
                out_ref[zd, k0 + b] = pltpu.einshape("ptl->p(tl)", jnp.stack(tiles)).astype(jnp.bfloat16)
        pltpu.make_async_copy(out_ref.at[zd], out_hbm.at[:, zd], sems.at[zd]).start()

    for zd in range(nsrc):
        pltpu.make_async_copy(out_ref.at[zd], out_hbm.at[:, zd], sems.at[zd]).wait()


def chi_kernel(scale, pos, im_ref, *refs):
    pieces, out_ref = refs[:8], refs[8]
    lower = lax.rem(lax.broadcasted_iota(jnp.int32, (32, LANES), 1), 64) < 32
    swapped = jnp.full((32, LANES), pos[2], jnp.int32) != 0
    for s in range(4):
        order = [lax.rem(pos[0] + 4 - x, 4) for x in range(4)]
        rhs = jnp.concatenate([pieces[2 * s + c][order[x]] for x in range(4) for c in range(2)], axis=0)
        acc = lax.dot_general(
            im_ref[...], rhs, (((1,), (1,)), ((), ())), preferred_element_type=jnp.float32
        )
        acc = acc * scale
        y = lax.rem(pos[1] + 4 - SHIFTS[s], 4)
        for xd in range(4):
            for h in range(2):
                tile = acc[32 * xd : 32 * xd + 32, LANES * h : LANES * h + LANES]
                turned = jnp.where(lower, pltpu.roll(tile, 96, 1), pltpu.roll(tile, 32, 1))
                out_ref[xd, 2 * y + h] = jnp.where(swapped, turned, tile).astype(jnp.bfloat16)


def local(three_centre, go_blocks, gv_blocks, go_index, gv_index, source_mask):
    pairs, aux, width = three_centre.shape
    nz = lax.axis_size("z")
    nx = lax.axis_size("x")
    number = pairs * nz
    blocks = go_blocks.shape[0]
    scale = float((number * width) ** -0.5)

    rows = pairs * BLK
    spread = pl.pallas_call(
        functools.partial(spread_kernel, blocks),
        out_shape=jax.ShapeDtypeStruct((nz, rows + 16, 4 * BLK), jnp.bfloat16),
        in_specs=[pl.BlockSpec(memory_space=pl.ANY)] * 4,
        out_specs=vmem(1)[0],
        scratch_shapes=[
            VMEM((pairs, aux, width), jnp.bfloat16),
            VMEM((3,) + go_index.shape, jnp.int32),
            VMEM((16, 4 * BLK), jnp.float32),
            pltpu.SemaphoreType.DMA((pairs,)),
            pltpu.SemaphoreType.DMA((3,)),
        ],
        name="spread",
    )(three_centre, go_index, gv_index, source_mask)
    w = lax.all_to_all(spread, "z", 0, 0, tiled=True)

    x = lax.axis_index("x")
    cx = []
    for s in range(nx):
        piece = lax.dynamic_index_in_dim(three_centre, lax.rem(x + s, nx), 0, keepdims=False)
        cx.append(piece if s == 0 else lax.ppermute(piece, "x", [(i, (i + s) % nx) for i in range(nx)]))
    cx = jnp.stack(cx)
    pieces = []
    for s in SHIFTS:
        own = cx if s == 0 else lax.ppermute(cx, "y", [(i, (i + s) % 4) for i in range(4)])
        pieces += [own, lax.ppermute(own, "core", [(0, 1), (1, 0)])]

    gt = go_blocks.reshape(blocks, 32, 2, 32, 2).transpose(0, 4, 3, 2, 1).reshape(blocks, BLK, BLK)
    zero = jnp.zeros_like(gv_blocks)
    vb = jnp.concatenate(
        [jnp.concatenate([gv_blocks, zero], axis=2), jnp.concatenate([zero, gv_blocks], axis=2)], axis=1
    )
    vb = jnp.concatenate([vb, jnp.zeros((1, LANES, LANES), jnp.bfloat16)], axis=0)

    got = w[:, rows : rows + 2 * pairs, :number].astype(jnp.int32)
    go_code = got[:, :pairs].reshape(number, number)
    gv_code = got[:, pairs:].reshape(number, number)
    image = pl.pallas_call(
        image_kernel,
        out_shape=jax.ShapeDtypeStruct((nx, nz, 4, width), jnp.bfloat16),
        in_specs=[pl.BlockSpec(memory_space=SMEM)] * 2 + vmem(3),
        out_specs=pl.BlockSpec(memory_space=pl.ANY),
        scratch_shapes=[VMEM((nz, nx, 4, width), jnp.bfloat16), pltpu.SemaphoreType.DMA((nz,))],
        compiler_params=pltpu.CompilerParams(vmem_limit_bytes=24 << 20),
        name="image",
    )(go_code, gv_code, w, gt, vb)
    image = lax.all_to_all(image.reshape(nx * nz, 4, width), ("x", "z"), 0, 0, tiled=True)

    part = pl.pallas_call(
        functools.partial(chi_kernel, scale),
        out_shape=jax.ShapeDtypeStruct((nx, nz, aux, 4 * aux), jnp.bfloat16),
        in_specs=[pl.BlockSpec(memory_space=SMEM)] + vmem(9),
        out_specs=vmem(1)[0],
        compiler_params=pltpu.CompilerParams(vmem_limit_bytes=24 << 20),
        name="chi",
    )(jnp.stack([x, lax.axis_index("y"), lax.axis_index("core")]), image.reshape(nx * nz * 4, width), *pieces)
    part = lax.all_to_all(part.reshape(nx * nz, aux, 4 * aux), ("x", "z"), 0, 0, tiled=True)
    return jnp.sum(part.astype(jnp.float32), axis=0)


def solution(mesh):
    grid = Mesh(mesh.devices.reshape(4, 4, 2, 8), WIDE + ("z",))
    rows = P("z", None)
    return jax.shard_map(
        local,
        mesh=grid,
        in_specs=(P("z", WIDE, None), P(), P(), rows, rows, rows),
        out_specs=P(WIDE, "z"),
        check_vma=False,
    )
```

```python
import functools

import jax
import jax.numpy as jnp
from jax import lax
from jax.experimental import pallas as pl
from jax.experimental.pallas import tpu as pltpu
from jax.sharding import Mesh, PartitionSpec as P

WIDE = ("y", "x", "core")
LANES = 128
BLK = 64
VMEM = pltpu.VMEM
SMEM = pltpu.SMEM
SHIFTS = (0, 1, 3, 2)


def vmem(n):
    return [pl.BlockSpec(memory_space=VMEM)] * n


def pair_halves(first, second):
    left = lax.broadcasted_iota(jnp.int32, first.shape, 1) < BLK
    low = jnp.where(left, first, pltpu.roll(second, BLK, 1))
    high = jnp.where(left, pltpu.roll(first, BLK, 1), second)
    return low, high


def spread_kernel(zero_code, c_hbm, go_hbm, gv_hbm, mask_hbm, out_ref, c_ref, ints, code, c_sem, int_sem):
    pairs, aux, width = c_ref.shape
    half = width // LANES
    loads = [pltpu.make_async_copy(c_hbm.at[j], c_ref.at[j], c_sem.at[j]) for j in range(pairs)]
    small = [pltpu.make_async_copy(ref, ints.at[i], int_sem.at[i]) for i, ref in enumerate((go_hbm, gv_hbm, mask_hbm))]
    for load in loads + small:
        load.start()
    for j in range(pairs):
        loads[j].wait()
        for g in range(aux // 16):
            x = c_ref[j, 16 * g : 16 * g + 16, :].astype(jnp.float32)
            x = pltpu.einshape("p(tl)->ptl", x, l=LANES)
            for i in range(4):
                d = 4 * g + i
                r = 2 * half * j
                for h in range(2):
                    one, two = x[4 * i + 2 * h], x[4 * i + 2 * h + 1]
                    low, high = pair_halves(one, two)
                    lanes = slice(LANES * h, LANES * h + LANES)
                    out_ref[d, r : r + half, lanes] = low.astype(jnp.bfloat16)
                    out_ref[d, r + half : r + 2 * half, lanes] = high.astype(jnp.bfloat16)
    rows = pairs * 2 * half
    number = ints.shape[2]
    for load in small:
        load.wait()
    code[...] = jnp.zeros_like(code)
    code[:pairs, :number] = ints[0].astype(jnp.float32)
    code[pairs : 2 * pairs, :number] = jnp.where(ints[2] != 0, ints[1], zero_code).astype(jnp.float32)
    for d in range(aux // 4):
        out_ref[d, rows : rows + 16, :] = code[...].astype(jnp.bfloat16)


def image_kernel(go_code, gv_code, w_ref, gt_ref, vb_ref, out_hbm, out_ref, stage, sems):
    nsrc = w_ref.shape[0]
    pairs = out_ref.shape[1]
    number = nsrc * pairs
    step, batch = 16, 4

    def finish(zd):
        for kk in range(pairs):
            out_ref[zd, kk] = pltpu.einshape("ptl->p(tl)", stage[kk]).astype(jnp.bfloat16)

    def send(zd):
        return pltpu.make_async_copy(out_ref.at[zd], out_hbm.at[:, zd], sems.at[zd])

    stage[...] = jnp.zeros_like(stage)

    @pl.loop(0, nsrc)
    def _(zd):
        finish(lax.max(zd - 1, 0))
        for k0 in range(0, pairs, batch):
            ks = [zd * pairs + k0 + b for b in range(batch)]
            accs = [None] * batch
            for jb in range(0, number, step):
                lefts, rights = [[] for _ in ks], [[] for _ in ks]
                for j in range(jb, jb + step):
                    r = BLK * (j % pairs)
                    gt = [gt_ref[go_code[k, j]] for k in ks]
                    first = jnp.dot(
                        gt[0] if batch == 1 else jnp.concatenate(gt, axis=0),
                        w_ref[j // pairs, r : r + BLK, :],
                        preferred_element_type=jnp.float32,
                    ).astype(jnp.bfloat16)
                    for b, k in enumerate(ks):
                        own = first[BLK * b : BLK * b + BLK]
                        lefts[b].append(jnp.concatenate([own[:, :LANES], own[:, LANES:]], axis=0))
                        rights[b].append(vb_ref[gv_code[k, j]])
                for b in range(batch):
                    part = jnp.dot(
                        jnp.concatenate(lefts[b], axis=1),
                        jnp.concatenate(rights[b], axis=0),
                        preferred_element_type=jnp.float32,
                    )
                    accs[b] = part if accs[b] is None else accs[b] + part
            for b, acc in enumerate(accs):
                for h in range(2):
                    tiles = pair_halves(acc[BLK * h : BLK * h + 32], acc[BLK * h + 32 : BLK * h + 64])
                    stage[k0 + b, 2 * h], stage[k0 + b, 2 * h + 1] = tiles

        @pl.when(zd > 0)
        def _():
            send(zd - 1).start()

    finish(nsrc - 1)
    send(nsrc - 1).start()
    for zd in range(nsrc):
        send(zd).wait()


def chi_kernel(scale, pos, im_ref, *refs):
    pieces, out_ref, rows = refs[:8], refs[8], refs[9]
    lower = lax.rem(lax.broadcasted_iota(jnp.int32, (32, LANES), 1), 64) < 32
    swapped = jnp.full((32, LANES), pos[2], jnp.int32) != 0
    for i in range(0, im_ref.shape[0], 4):
        four = [im_ref[i + b].astype(jnp.float32) for b in range(4)]
        rows[4 * i : 4 * i + 16, :] = jnp.concatenate(four, axis=0).astype(jnp.bfloat16)
    order = [lax.rem(pos[0] + 4 - x, 4) for x in range(4)]
    for s in range(4):
        rhs = jnp.concatenate([pieces[2 * s + c][order[x]] for x in range(4) for c in range(2)], axis=0)
        acc = lax.dot_general(rows[...], rhs, (((1,), (1,)), ((), ())), preferred_element_type=jnp.float32)
        acc = acc * scale
        y = lax.rem(pos[1] + 4 - SHIFTS[s], 4)
        for xd in range(4):
            for h in range(2):
                tile = acc[32 * xd : 32 * xd + 32, LANES * h : LANES * h + LANES]
                turned = jnp.where(lower, pltpu.roll(tile, 96, 1), pltpu.roll(tile, 32, 1))
                out_ref[xd, 2 * y + h] = jnp.where(swapped, turned, tile).astype(jnp.bfloat16)


def local(three_centre, go_blocks, gv_blocks, go_index, gv_index, source_mask):
    pairs, aux, width = three_centre.shape
    nz = lax.axis_size("z")
    nx = lax.axis_size("x")
    number = pairs * nz
    blocks = go_blocks.shape[0]
    scale = float((number * width) ** -0.5)

    rows = pairs * BLK
    spread = pl.pallas_call(
        functools.partial(spread_kernel, blocks),
        out_shape=jax.ShapeDtypeStruct((nz, rows + 16, 4 * BLK), jnp.bfloat16),
        in_specs=[pl.BlockSpec(memory_space=pl.ANY)] * 4,
        out_specs=vmem(1)[0],
        scratch_shapes=[
            VMEM((pairs, aux, width), jnp.bfloat16),
            VMEM((3,) + go_index.shape, jnp.int32),
            VMEM((16, 4 * BLK), jnp.float32),
            pltpu.SemaphoreType.DMA((pairs,)),
            pltpu.SemaphoreType.DMA((3,)),
        ],
        name="spread",
    )(three_centre, go_index, gv_index, source_mask)
    w = lax.all_to_all(spread, "z", 0, 0, tiled=True)

    x = lax.axis_index("x")
    cx = []
    for s in range(nx):
        piece = lax.dynamic_index_in_dim(three_centre, lax.rem(x + s, nx), 0, keepdims=False)
        cx.append(piece if s == 0 else lax.ppermute(piece, "x", [(i, (i + s) % nx) for i in range(nx)]))
    cx = jnp.stack(cx)
    pieces = []
    for s in SHIFTS:
        own = cx if s == 0 else lax.ppermute(cx, "y", [(i, (i + s) % 4) for i in range(4)])
        pieces += [own, lax.ppermute(own, "core", [(0, 1), (1, 0)])]

    gt = go_blocks.reshape(blocks, 32, 2, 32, 2).transpose(0, 4, 3, 2, 1).reshape(blocks, BLK, BLK)
    zero = jnp.zeros_like(gv_blocks)
    vb = jnp.concatenate(
        [jnp.concatenate([gv_blocks, zero], axis=2), jnp.concatenate([zero, gv_blocks], axis=2)], axis=1
    )
    vb = jnp.concatenate([vb, jnp.zeros((1, LANES, LANES), jnp.bfloat16)], axis=0)

    got = w[:, rows : rows + 2 * pairs, :number].astype(jnp.int32)
    go_code = got[:, :pairs].reshape(number, number)
    gv_code = got[:, pairs:].reshape(number, number)
    image = pl.pallas_call(
        image_kernel,
        out_shape=jax.ShapeDtypeStruct((nx, nz, 4, width), jnp.bfloat16),
        in_specs=[pl.BlockSpec(memory_space=SMEM)] * 2 + vmem(3),
        out_specs=pl.BlockSpec(memory_space=pltpu.HBM),
        scratch_shapes=[
            VMEM((nz, nx, 4, width), jnp.bfloat16),
            VMEM((pairs, 4, width // LANES, LANES), jnp.float32),
            pltpu.SemaphoreType.DMA((nz,)),
        ],
        compiler_params=pltpu.CompilerParams(vmem_limit_bytes=24 << 20),
        name="image",
    )(go_code, gv_code, w, gt, vb)
    image = lax.all_to_all(image.reshape(nx * nz, 4, width), ("x", "z"), 0, 0, tiled=True)

    part = pl.pallas_call(
        functools.partial(chi_kernel, scale),
        out_shape=jax.ShapeDtypeStruct((nx, nz, aux, 4 * aux), jnp.bfloat16),
        in_specs=[pl.BlockSpec(memory_space=SMEM)] + vmem(9),
        out_specs=vmem(1)[0],
        scratch_shapes=[VMEM((nx * nz * 4, width), jnp.bfloat16)],
        compiler_params=pltpu.CompilerParams(vmem_limit_bytes=24 << 20),
        name="chi",
    )(jnp.stack([x, lax.axis_index("y"), lax.axis_index("core")]), image, *pieces)
    part = lax.all_to_all(part.reshape(nx * nz, aux, 4 * aux), ("x", "z"), 0, 0, tiled=True)
    return jnp.sum(part.astype(jnp.float32), axis=0)


def solution(mesh):
    grid = Mesh(mesh.devices.reshape(4, 4, 2, 8), WIDE + ("z",))
    rows = P("z", None)
    return jax.shard_map(
        local,
        mesh=grid,
        in_specs=(P("z", WIDE, None), P(), P(), rows, rows, rows),
        out_specs=P(WIDE, "z"),
        check_vma=False,
    )
```

```python
import functools

import jax
import jax.numpy as jnp
from jax import lax
from jax.experimental import pallas as pl
from jax.experimental.pallas import tpu as pltpu
from jax.sharding import Mesh, PartitionSpec as P

WIDE = ("y", "x", "core")
LANES = 128
BLK = 64
VMEM = pltpu.VMEM
SMEM = pltpu.SMEM
SHIFTS = (0, 1, 3, 2)


def vmem(n):
    return [pl.BlockSpec(memory_space=VMEM)] * n


def pair_halves(first, second):
    left = lax.broadcasted_iota(jnp.int32, first.shape, 1) < BLK
    low = jnp.where(left, first, pltpu.roll(second, BLK, 1))
    high = jnp.where(left, pltpu.roll(first, BLK, 1), second)
    return low, high


def spread_kernel(zero_code, c_hbm, go_hbm, gv_hbm, mask_hbm, out_ref, c_ref, ints, code, c_sem, int_sem):
    pairs, aux, width = c_ref.shape
    half = width // LANES
    loads = [pltpu.make_async_copy(c_hbm.at[j], c_ref.at[j], c_sem.at[j]) for j in range(pairs)]
    small = [pltpu.make_async_copy(ref, ints.at[i], int_sem.at[i]) for i, ref in enumerate((go_hbm, gv_hbm, mask_hbm))]
    for load in loads + small:
        load.start()
    for j in range(pairs):
        loads[j].wait()
        for g in range(aux // 16):
            x = c_ref[j, 16 * g : 16 * g + 16, :].astype(jnp.float32)
            x = pltpu.einshape("p(tl)->ptl", x, l=LANES)
            for i in range(4):
                d = 4 * g + i
                r = 2 * half * j
                for h in range(2):
                    one, two = x[4 * i + 2 * h], x[4 * i + 2 * h + 1]
                    low, high = pair_halves(one, two)
                    lanes = slice(LANES * h, LANES * h + LANES)
                    out_ref[d, r : r + half, lanes] = low.astype(jnp.bfloat16)
                    out_ref[d, r + half : r + 2 * half, lanes] = high.astype(jnp.bfloat16)
    rows = pairs * 2 * half
    number = ints.shape[2]
    for load in small:
        load.wait()
    code[...] = jnp.zeros_like(code)
    code[:pairs, :number] = ints[0].astype(jnp.float32)
    code[pairs : 2 * pairs, :number] = jnp.where(ints[2] != 0, ints[1], zero_code).astype(jnp.float32)
    for d in range(aux // 4):
        out_ref[d, rows : rows + 16, :] = code[...].astype(jnp.bfloat16)


def image_kernel(go_code, gv_code, w_ref, gt_ref, vb_ref, out_hbm, out_ref, stage, sems):
    nsrc = w_ref.shape[0]
    pairs = out_ref.shape[1]
    number = nsrc * pairs
    step, batch = 16, 2

    def finish(zd):
        for kk in range(pairs):
            out_ref[zd, kk] = pltpu.einshape("ptl->p(tl)", stage[kk]).astype(jnp.bfloat16)

    def send(zd):
        return pltpu.make_async_copy(out_ref.at[zd], out_hbm.at[:, zd], sems.at[zd])

    stage[...] = jnp.zeros_like(stage)

    @pl.loop(0, nsrc)
    def _(zd):
        finish(lax.max(zd - 1, 0))
        for k0 in range(0, pairs, batch):
            ks = [zd * pairs + k0 + b for b in range(batch)]
            accs = [None] * batch
            for jb in range(0, number, step):
                lefts, rights = [[] for _ in ks], [[] for _ in ks]
                for j in range(jb, jb + step):
                    r = BLK * (j % pairs)
                    gt = [gt_ref[go_code[k, j]] for k in ks]
                    first = jnp.dot(
                        gt[0] if batch == 1 else jnp.concatenate(gt, axis=0),
                        w_ref[j // pairs, r : r + BLK, :],
                        preferred_element_type=jnp.float32,
                    ).astype(jnp.bfloat16)
                    for b, k in enumerate(ks):
                        own = first[BLK * b : BLK * b + BLK]
                        lefts[b].append(jnp.concatenate([own[:, :LANES], own[:, LANES:]], axis=0))
                        rights[b].append(vb_ref[gv_code[k, j]])
                for b in range(batch):
                    part = jnp.dot(
                        jnp.concatenate(lefts[b], axis=1),
                        jnp.concatenate(rights[b], axis=0),
                        preferred_element_type=jnp.float32,
                    )
                    accs[b] = part if accs[b] is None else accs[b] + part
            for b, acc in enumerate(accs):
                for h in range(2):
                    tiles = pair_halves(acc[BLK * h : BLK * h + 32], acc[BLK * h + 32 : BLK * h + 64])
                    stage[k0 + b, 2 * h], stage[k0 + b, 2 * h + 1] = tiles

        @pl.when(zd > 0)
        def _():
            send(zd - 1).start()

    finish(nsrc - 1)
    send(nsrc - 1).start()
    for zd in range(nsrc):
        send(zd).wait()


def chi_kernel(scale, pos, im_ref, *refs):
    pieces, out_ref, rows = refs[:8], refs[8], refs[9]
    lower = lax.rem(lax.broadcasted_iota(jnp.int32, (32, LANES), 1), 64) < 32
    swapped = jnp.full((32, LANES), pos[2], jnp.int32) != 0
    for i in range(0, im_ref.shape[0], 4):
        four = [im_ref[i + b].astype(jnp.float32) for b in range(4)]
        rows[4 * i : 4 * i + 16, :] = jnp.concatenate(four, axis=0).astype(jnp.bfloat16)
    order = [lax.rem(pos[0] + 4 - x, 4) for x in range(4)]
    for s in range(4):
        rhs = jnp.concatenate([pieces[2 * s + c][order[x]] for x in range(4) for c in range(2)], axis=0)
        acc = lax.dot_general(rows[...], rhs, (((1,), (1,)), ((), ())), preferred_element_type=jnp.float32)
        acc = acc * scale
        y = lax.rem(pos[1] + 4 - SHIFTS[s], 4)
        for xd in range(4):
            for h in range(2):
                tile = acc[32 * xd : 32 * xd + 32, LANES * h : LANES * h + LANES]
                turned = jnp.where(lower, pltpu.roll(tile, 96, 1), pltpu.roll(tile, 32, 1))
                out_ref[xd, 2 * y + h] = jnp.where(swapped, turned, tile).astype(jnp.bfloat16)


def local(three_centre, go_blocks, gv_blocks, go_index, gv_index, source_mask):
    pairs, aux, width = three_centre.shape
    nz = lax.axis_size("z")
    nx = lax.axis_size("x")
    number = pairs * nz
    blocks = go_blocks.shape[0]
    scale = float((number * width) ** -0.5)

    rows = pairs * BLK
    spread = pl.pallas_call(
        functools.partial(spread_kernel, blocks),
        out_shape=jax.ShapeDtypeStruct((nz, rows + 16, 4 * BLK), jnp.bfloat16),
        in_specs=[pl.BlockSpec(memory_space=pl.ANY)] * 4,
        out_specs=vmem(1)[0],
        scratch_shapes=[
            VMEM((pairs, aux, width), jnp.bfloat16),
            VMEM((3,) + go_index.shape, jnp.int32),
            VMEM((16, 4 * BLK), jnp.float32),
            pltpu.SemaphoreType.DMA((pairs,)),
            pltpu.SemaphoreType.DMA((3,)),
        ],
        name="spread",
    )(three_centre, go_index, gv_index, source_mask)
    w = lax.all_to_all(spread, "z", 0, 0, tiled=True)

    x = lax.axis_index("x")
    cx = []
    for s in range(nx):
        piece = lax.dynamic_index_in_dim(three_centre, lax.rem(x + s, nx), 0, keepdims=False)
        cx.append(piece if s == 0 else lax.ppermute(piece, "x", [(i, (i + s) % nx) for i in range(nx)]))
    cx = jnp.stack(cx)
    pieces = []
    for s in SHIFTS:
        own = cx if s == 0 else lax.ppermute(cx, "y", [(i, (i + s) % 4) for i in range(4)])
        pieces += [own, lax.ppermute(own, "core", [(0, 1), (1, 0)])]

    gt = go_blocks.reshape(blocks, 32, 2, 32, 2).transpose(0, 4, 3, 2, 1).reshape(blocks, BLK, BLK)
    zero = jnp.zeros_like(gv_blocks)
    vb = jnp.concatenate(
        [jnp.concatenate([gv_blocks, zero], axis=2), jnp.concatenate([zero, gv_blocks], axis=2)], axis=1
    )
    vb = jnp.concatenate([vb, jnp.zeros((1, LANES, LANES), jnp.bfloat16)], axis=0)

    got = w[:, rows : rows + 2 * pairs, :number].astype(jnp.int32)
    go_code = got[:, :pairs].reshape(number, number)
    gv_code = got[:, pairs:].reshape(number, number)
    image = pl.pallas_call(
        image_kernel,
        out_shape=jax.ShapeDtypeStruct((nx, nz, 4, width), jnp.bfloat16),
        in_specs=[pl.BlockSpec(memory_space=SMEM)] * 2 + vmem(3),
        out_specs=pl.BlockSpec(memory_space=pltpu.HBM),
        scratch_shapes=[
            VMEM((nz, nx, 4, width), jnp.bfloat16),
            VMEM((pairs, 4, width // LANES, LANES), jnp.float32),
            pltpu.SemaphoreType.DMA((nz,)),
        ],
        compiler_params=pltpu.CompilerParams(vmem_limit_bytes=60 << 20),
        name="image",
    )(go_code, gv_code, w, gt, vb)
    image = lax.all_to_all(image.reshape(nx * nz, 4, width), ("x", "z"), 0, 0, tiled=True)

    part = pl.pallas_call(
        functools.partial(chi_kernel, scale),
        out_shape=jax.ShapeDtypeStruct((nx, nz, aux, 4 * aux), jnp.bfloat16),
        in_specs=[pl.BlockSpec(memory_space=SMEM)] + vmem(9),
        out_specs=vmem(1)[0],
        scratch_shapes=[VMEM((nx * nz * 4, width), jnp.bfloat16)],
        compiler_params=pltpu.CompilerParams(vmem_limit_bytes=24 << 20),
        name="chi",
    )(jnp.stack([x, lax.axis_index("y"), lax.axis_index("core")]), image, *pieces)
    part = lax.all_to_all(part.reshape(nx * nz, aux, 4 * aux), ("x", "z"), 0, 0, tiled=True)
    return jnp.sum(part.astype(jnp.float32), axis=0)


def solution(mesh):
    grid = Mesh(mesh.devices.reshape(4, 4, 2, 8), WIDE + ("z",))
    rows = P("z", None)
    return jax.shard_map(
        local,
        mesh=grid,
        in_specs=(P("z", WIDE, None), P(), P(), rows, rows, rows),
        out_specs=P(WIDE, "z"),
        check_vma=False,
    )
```

```python
import functools

import jax
import jax.numpy as jnp
from jax import lax
from jax.experimental import pallas as pl
from jax.experimental.pallas import tpu as pltpu
from jax.sharding import Mesh, PartitionSpec as P

WIDE = ("y", "x", "core")
LANES = 128
BLK = 64
VMEM = pltpu.VMEM
SMEM = pltpu.SMEM
SHIFTS = (0, 1, 3, 2)


def vmem(n):
    return [pl.BlockSpec(memory_space=VMEM)] * n


def pair_halves(first, second):
    left = lax.broadcasted_iota(jnp.int32, first.shape, 1) < BLK
    low = jnp.where(left, first, pltpu.roll(second, BLK, 1))
    high = jnp.where(left, pltpu.roll(first, BLK, 1), second)
    return low, high


def spread_kernel(zero_code, c_hbm, go_hbm, gv_hbm, mask_hbm, out_ref, c_ref, ints, code, c_sem, int_sem):
    pairs, aux, width = c_ref.shape
    half = width // LANES
    loads = [pltpu.make_async_copy(c_hbm.at[j], c_ref.at[j], c_sem.at[j]) for j in range(pairs)]
    small = [pltpu.make_async_copy(ref, ints.at[i], int_sem.at[i]) for i, ref in enumerate((go_hbm, gv_hbm, mask_hbm))]
    for load in loads + small:
        load.start()
    for j in range(pairs):
        loads[j].wait()
        for g in range(aux // 16):
            x = c_ref[j, 16 * g : 16 * g + 16, :].astype(jnp.float32)
            x = pltpu.einshape("p(tl)->ptl", x, l=LANES)
            for i in range(4):
                d = 4 * g + i
                r = 2 * half * j
                for h in range(2):
                    one, two = x[4 * i + 2 * h], x[4 * i + 2 * h + 1]
                    low, high = pair_halves(one, two)
                    lanes = slice(LANES * h, LANES * h + LANES)
                    out_ref[d, r : r + half, lanes] = low.astype(jnp.bfloat16)
                    out_ref[d, r + half : r + 2 * half, lanes] = high.astype(jnp.bfloat16)
    rows = pairs * 2 * half
    number = ints.shape[2]
    for load in small:
        load.wait()
    code[...] = jnp.zeros_like(code)
    code[:pairs, :number] = ints[0].astype(jnp.float32)
    code[pairs : 2 * pairs, :number] = jnp.where(ints[2] != 0, ints[1], zero_code).astype(jnp.float32)
    for d in range(aux // 4):
        out_ref[d, rows : rows + 16, :] = code[...].astype(jnp.bfloat16)


def image_kernel(go_code, gv_code, w_ref, gt_ref, vb_ref, out_hbm, out_ref, stage, sems):
    nsrc = w_ref.shape[0]
    pairs = out_ref.shape[1]
    number = nsrc * pairs
    step, batch = 16, 2

    def finish(zd):
        for kk in range(pairs):
            out_ref[zd, kk] = pltpu.einshape("ptl->p(tl)", stage[kk]).astype(jnp.bfloat16)

    def send(zd):
        return pltpu.make_async_copy(out_ref.at[zd], out_hbm.at[:, zd], sems.at[zd])

    stage[...] = jnp.zeros_like(stage)

    @pl.loop(0, nsrc)
    def _(zd):
        finish(lax.max(zd - 1, 0))
        for k0 in range(0, pairs, batch):
            ks = [zd * pairs + k0 + b for b in range(batch)]
            accs = [None] * batch
            for jb in range(0, number, step):
                lefts, rights = [[] for _ in ks], [[] for _ in ks]
                for j in range(jb, jb + step):
                    r = BLK * (j % pairs)
                    gt = [gt_ref[go_code[k, j]] for k in ks]
                    first = jnp.dot(
                        gt[0] if batch == 1 else jnp.concatenate(gt, axis=0),
                        w_ref[j // pairs, r : r + BLK, :],
                        preferred_element_type=jnp.float32,
                    ).astype(jnp.bfloat16)
                    for b, k in enumerate(ks):
                        own = first[BLK * b : BLK * b + BLK]
                        lefts[b].append(jnp.concatenate([own[:, :LANES], own[:, LANES:]], axis=0))
                        rights[b].append(vb_ref[gv_code[k, j]])
                for b in range(batch):
                    part = jnp.dot(
                        jnp.concatenate(lefts[b], axis=1),
                        jnp.concatenate(rights[b], axis=0),
                        preferred_element_type=jnp.float32,
                    )
                    accs[b] = part if accs[b] is None else accs[b] + part
            for b, acc in enumerate(accs):
                for h in range(2):
                    tiles = pair_halves(acc[BLK * h : BLK * h + 32], acc[BLK * h + 32 : BLK * h + 64])
                    stage[k0 + b, 2 * h], stage[k0 + b, 2 * h + 1] = tiles

        @pl.when(zd > 0)
        def _():
            send(zd - 1).start()

    finish(nsrc - 1)
    send(nsrc - 1).start()
    for zd in range(nsrc):
        send(zd).wait()


def chi_kernel(scale, pos, im_ref, *refs):
    pieces, out_ref, rows = refs[:8], refs[8], refs[9]
    lower = lax.rem(lax.broadcasted_iota(jnp.int32, (32, LANES), 1), 64) < 32
    swapped = jnp.full((32, LANES), pos[2], jnp.int32) != 0
    for i in range(0, im_ref.shape[0], 4):
        four = [im_ref[i + b].astype(jnp.float32) for b in range(4)]
        rows[4 * i : 4 * i + 16, :] = jnp.concatenate(four, axis=0).astype(jnp.bfloat16)
    order = [lax.rem(pos[0] + 4 - x, 4) for x in range(4)]
    for s in range(4):
        rhs = jnp.concatenate([pieces[2 * s + c][order[x]] for x in range(4) for c in range(2)], axis=0)
        acc = lax.dot_general(rows[...], rhs, (((1,), (1,)), ((), ())), preferred_element_type=jnp.float32)
        acc = acc * scale
        y = lax.rem(pos[1] + 4 - SHIFTS[s], 4)
        for xd in range(4):
            for h in range(2):
                tile = acc[32 * xd : 32 * xd + 32, LANES * h : LANES * h + LANES]
                turned = jnp.where(lower, pltpu.roll(tile, 96, 1), pltpu.roll(tile, 32, 1))
                out_ref[xd, 2 * y + h] = jnp.where(swapped, turned, tile).astype(jnp.bfloat16)


def local(three_centre, go_blocks, gv_blocks, go_index, gv_index, source_mask):
    pairs, aux, width = three_centre.shape
    nz = lax.axis_size("z")
    nx = lax.axis_size("x")
    number = pairs * nz
    blocks = go_blocks.shape[0]
    scale = float((number * width) ** -0.5)

    rows = pairs * BLK
    spread = pl.pallas_call(
        functools.partial(spread_kernel, blocks),
        out_shape=jax.ShapeDtypeStruct((nz, rows + 16, 4 * BLK), jnp.bfloat16),
        in_specs=[pl.BlockSpec(memory_space=pl.ANY)] * 4,
        out_specs=vmem(1)[0],
        scratch_shapes=[
            VMEM((pairs, aux, width), jnp.bfloat16),
            VMEM((3,) + go_index.shape, jnp.int32),
            VMEM((16, 4 * BLK), jnp.float32),
            pltpu.SemaphoreType.DMA((pairs,)),
            pltpu.SemaphoreType.DMA((3,)),
        ],
        name="spread",
    )(three_centre, go_index, gv_index, source_mask)
    w = lax.all_to_all(spread, "z", 0, 0, tiled=True)

    x = lax.axis_index("x")
    cx = []
    for s in range(nx):
        piece = lax.dynamic_index_in_dim(three_centre, lax.rem(x + s, nx), 0, keepdims=False)
        cx.append(piece if s == 0 else lax.ppermute(piece, "x", [(i, (i + s) % nx) for i in range(nx)]))
    cx = jnp.stack(cx)
    pieces = []
    for s in SHIFTS:
        own = cx if s == 0 else lax.ppermute(cx, "y", [(i, (i + s) % 4) for i in range(4)])
        pieces += [own, lax.ppermute(own, "core", [(0, 1), (1, 0)])]

    gt = go_blocks.reshape(blocks, 32, 2, 32, 2).transpose(0, 4, 3, 2, 1).reshape(blocks, BLK, BLK)
    zero = jnp.zeros_like(gv_blocks)
    vb = jnp.concatenate(
        [jnp.concatenate([gv_blocks, zero], axis=2), jnp.concatenate([zero, gv_blocks], axis=2)], axis=1
    )
    vb = jnp.concatenate([vb, jnp.zeros((1, LANES, LANES), jnp.bfloat16)], axis=0)

    got = w[:, rows : rows + 2 * pairs, :number].astype(jnp.int32)
    go_code = got[:, :pairs].reshape(number, number)
    gv_code = got[:, pairs:].reshape(number, number)
    image = pl.pallas_call(
        image_kernel,
        out_shape=jax.ShapeDtypeStruct((nx, nz, 4, width), jnp.bfloat16),
        in_specs=[pl.BlockSpec(memory_space=SMEM)] * 2 + vmem(3),
        out_specs=pl.BlockSpec(memory_space=pltpu.HBM),
        scratch_shapes=[
            VMEM((nz, nx, 4, width), jnp.bfloat16),
            VMEM((pairs, 4, width // LANES, LANES), jnp.float32),
            pltpu.SemaphoreType.DMA((nz,)),
        ],
        compiler_params=pltpu.CompilerParams(vmem_limit_bytes=24 << 20),
        name="image",
    )(go_code, gv_code, w, gt, vb)
    image = lax.all_to_all(image.reshape(nx * nz, 4, width), ("x", "z"), 0, 0, tiled=True)

    part = pl.pallas_call(
        functools.partial(chi_kernel, scale),
        out_shape=jax.ShapeDtypeStruct((nx, nz, aux, 4 * aux), jnp.bfloat16),
        in_specs=[pl.BlockSpec(memory_space=SMEM)] + vmem(9),
        out_specs=vmem(1)[0],
        scratch_shapes=[VMEM((nx * nz * 4, width), jnp.bfloat16)],
        compiler_params=pltpu.CompilerParams(vmem_limit_bytes=24 << 20),
        name="chi",
    )(jnp.stack([x, lax.axis_index("y"), lax.axis_index("core")]), image, *pieces)
    part = lax.all_to_all(part.reshape(nx * nz, aux, 4 * aux), ("x", "z"), 0, 0, tiled=True)
    return jnp.sum(part.astype(jnp.float32), axis=0)


def solution(mesh):
    grid = Mesh(mesh.devices.reshape(4, 4, 2, 8), WIDE + ("z",))
    rows = P("z", None)
    return jax.shard_map(
        local,
        mesh=grid,
        in_specs=(P("z", WIDE, None), P(), P(), rows, rows, rows),
        out_specs=P(WIDE, "z"),
        check_vma=False,
    )
```
